512 devices in a mesh: section: 16 (over z_lo, y), shard: 32 (over x, z_hi, core).
Axes of the slice: x: 4, y: 8, z: 8 (z_hi: 4, z_lo: 2; z = z_hi * 2 + z_lo), core: 2. Of those that a mesh axis runs over, the one named last changes fastest.
Arguments:
- layer_input: bfloat16 [16, 4096, 3072], P('section', 'shard'), may hold values from -150 to 150
- out_grad: bfloat16 [16, 4096, 3072], P('section', 'shard'), may hold values from -60 to 60
- modulation: float32 [16, 4, 3, 3072], P('section'), may hold values from -3 to 3
- proj_weight: bfloat16 [16, 3072, 3072], P('section', 'shard'), may hold values from -0.109375 to 0.109375
Outputs:
- handoff: bfloat16 [16, 4096, 3072], P('section', 'shard')
- mod_grad: float32 [16, 4, 3, 3072], P('section')
The draws below stay inside these ranges and needn't reach their ends.
All inputs are finite; a program needn't handle non-finite values.
Results may differ from the reference program's by a relative error of at most 0.0029.
Values may be sent and summed in bfloat16 or wider, within the bound.
A program may use at most 128 MiB of HBM per device.

```python
import math
import jax
import jax.numpy as jnp
from jax import lax

DW = 3072
SEQS = 4
TOKENS = 4096
SECTIONS = 16


def draw_layer_input(key, part):
    first, second, third = jax.random.split(jax.random.fold_in(key, 11), 3)
    shape = (SECTIONS, TOKENS, DW)
    base = jnp.clip(jax.random.normal(first, shape, jnp.float32), -5.0, 5.0)
    row_scale = jnp.exp(jax.random.uniform(second, (SECTIONS, TOKENS, 1), jnp.float32) * math.log(10.0))
    col_scale = jnp.exp(jax.random.uniform(third, (1, 1, DW), jnp.float32, -1.0, 1.0) * math.log(3.0))
    return (base * row_scale * col_scale).astype(jnp.bfloat16)


def draw_out_grad(key, part):
    first, second = jax.random.split(jax.random.fold_in(key, 23), 2)
    shape = (SECTIONS, TOKENS, DW)
    base = jnp.clip(jax.random.normal(first, shape, jnp.float32), -5.0, 5.0)
    row_scale = jnp.exp(jax.random.uniform(second, (SECTIONS, TOKENS, 1), jnp.float32) * math.log(4.0))
    rising = jnp.exp(jnp.arange(TOKENS, dtype=jnp.float32) / TOKENS * math.log(3.0))
    return (base * row_scale * rising[None, :, None]).astype(jnp.bfloat16)


def block_levels(rng, dims, cuts, smallest, high):
    level, own = 1.0, jax.random.fold_in(rng, 6)
    for position, shards_of in cuts:
        heights = jnp.exp(jax.random.uniform(jax.random.fold_in(own, position), (shards_of,), jnp.float32, smallest / len(cuts), high / len(cuts)))
        level = level * jnp.repeat(heights, dims[position] // shards_of).reshape([-1 if axis == position else 1 for axis in range(len(dims))])
    return level


def noise(rng, shape, scale, limit, cuts=(), kind=jnp.bfloat16):
    drawn = jax.random.normal(rng, shape, jnp.float32) * scale
    if len(cuts) > 0:
        drawn = block_levels(rng, shape, cuts, -0.22, 0.18) * drawn
    return jnp.clip(drawn, min=-limit, max=limit).astype(kind)


def setup_inputs(seed: int = 0) -> dict:
    streams_of = jax.random.split(jax.random.key(seed), 5)
    return {
        "layer_input": draw_layer_input(jax.random.fold_in(streams_of[4], 71), 0),
        "out_grad": draw_out_grad(jax.random.fold_in(streams_of[4], 71), 0),
        "modulation": noise(streams_of[2], (SECTIONS, SEQS, 3, DW), 0.5, 3.0, ((0, 16),), jnp.float32),
        "proj_weight": noise(streams_of[3], (SECTIONS, DW, DW), DW ** -0.5, 0.109375, ((0, 16), (1, 32))),
    }


def modulate_rows(token_ids, seq_length, mod_table):
    sample = token_ids // seq_length
    select = (sample[:, None] == jnp.arange(SEQS)[None, :]).astype(jnp.float32)
    per_row = jnp.einsum('rs,skd->rkd', select, mod_table, precision=lax.Precision.HIGHEST)
    return (select, per_row)

def norm_rows(activation):
    values = activation.astype(jnp.float32)
    center = values - lax.optimization_barrier(jnp.mean(values, axis=-1, keepdims=True))
    variance = lax.optimization_barrier(jnp.mean(center * center, axis=-1, keepdims=True))
    inv_scale = lax.rsqrt(variance + 1e-06)
    return (center * inv_scale, inv_scale)

def section_backward(section_args):
    activation, grad_out, mod_table, weight = section_args
    row_count = activation.shape[0]
    seq_length = row_count // SEQS
    select, per_row = modulate_rows(jnp.arange(row_count), seq_length, mod_table)
    normed, inv_scale = norm_rows(activation)
    modulated = (normed * (1.0 + per_row[:, 1]) + per_row[:, 0]).astype(jnp.bfloat16)
    branch = jnp.dot(modulated, weight, preferred_element_type=jnp.float32)
    grad_values = grad_out.astype(jnp.float32)
    scaled_grad = (per_row[:, 2] * grad_values).astype(jnp.bfloat16)
    grad_mod = jnp.dot(scaled_grad, weight.T, preferred_element_type=jnp.float32)
    grad_gate = jnp.einsum('rs,rd->sd', select, grad_values * branch, precision=lax.Precision.HIGHEST)
    grad_shift = jnp.einsum('rs,rd->sd', select, grad_mod, precision=lax.Precision.HIGHEST)
    grad_scale = jnp.einsum('rs,rd->sd', select, grad_mod * normed, precision=lax.Precision.HIGHEST)
    grad_norm = grad_mod * (1.0 + per_row[:, 1])
    centered = grad_norm - lax.optimization_barrier(jnp.mean(grad_norm, axis=-1, keepdims=True))
    grad_in = grad_values + inv_scale * (centered - normed * lax.optimization_barrier(jnp.mean(grad_norm * normed, axis=-1, keepdims=True)))
    return (grad_in.astype(jnp.bfloat16), jnp.stack([grad_shift, grad_scale, grad_gate], axis=1))

def reference(layer_input, out_grad, modulation, proj_weight):
    grads, mod_grad = lax.map(section_backward, (layer_input, out_grad, modulation, proj_weight))
    handoff = jnp.concatenate([grads[1:], jnp.zeros_like(grads[:1])], axis=0)
    return (handoff, mod_grad)
```

```python
import functools

import jax
import jax.numpy as jnp
from jax import lax
from jax.experimental import pallas as pl
from jax.experimental.pallas import tpu as pltpu
from jax.sharding import PartitionSpec as P

MESH = pl.DeviceIdType.MESH
F32 = jnp.float32
BF16 = jnp.bfloat16

SEQS = 4
OFF = (0, 3, 1, 2)
AWAY = (0, 1, 3, 2)
LANES = 128
COPIES = 64


def stats_to_rows(first, second):
    lane = lax.broadcasted_iota(jnp.int32, (LANES, LANES), 1)
    square = jnp.where(lane == 0, first, jnp.where(lane == 1, second, 0.0))
    return jnp.transpose(square)[:8]


def rows_to_stats(rows):
    square = jnp.concatenate([rows, jnp.zeros((LANES - 8, LANES), F32)], axis=0)
    columns = jnp.transpose(square)
    return columns[:, 0:1], columns[:, 1:2]


def kernel(
    sections, li_ref, og_ref, mod_ref, w_ref, out_ref, mg_ref,
    og_all, li_all, w_all, st_all, scaled, normed, inv_all, modulated, gm, gn, outgoing,
    gate_acc, sums, part, gate_buf, gate_rx, rs, full, send_sem, recv_sem, local_sem,
):
    rows, feats = og_ref.shape
    block = feats // 4
    chunk = feats // 16
    w_rows = w_ref.shape[0]
    owners = block // LANES
    half, w_half = rows // 2, w_rows // 2

    sec = lax.axis_index("section")
    shard = lax.axis_index("shard")
    x = shard // 8
    z = (shard % 8) // 2
    c = shard % 2
    other = 1 - c

    def at_x(k):
        return (sec, lax.rem(x + k, 4) * 8 + z * 2 + c)

    def at_z(dz, dc):
        return (sec, x * 8 + lax.rem(z + dz, 4) * 2 + lax.rem(c + dc, 2))

    def at_section(step, pos):
        return (sec + step, pos * 8 + z * 2 + c)

    def copy(ident, src, dst, device):
        return pltpu.make_async_remote_copy(
            src_ref=src, dst_ref=dst, send_sem=send_sem.at[ident], recv_sem=recv_sem.at[ident],
            device_id=device, device_id_type=MESH,
        )

    ids = iter(range(COPIES))
    slot_x = [lax.rem(x + OFF[n], 4) for n in range(4)]
    group = [(dz, dc) for dz in range(4) for dc in range(2) if (dz, dc) != (0, 0)]

    def columns(pos):
        return pl.ds(pl.multiple_of(pos * block, LANES), block)

    own_columns = columns(x)

    barrier = pltpu.get_barrier_semaphore()

    def greet(device):
        pl.semaphore_signal(barrier, inc=1, device_id=device, device_id_type=MESH)

    for k in range(1, 4):
        greet(at_x(k))
    for dz, dc in group:
        greet(at_z(dz, dc))

    @pl.when(sec > 0)
    def _():
        for pos in range(4):
            greet(at_section(-1, pos))

    @pl.when(sec < sections - 1)
    def _():
        for pos in range(4):
            greet(at_section(1, pos))

    neighbours = (sec + sections - 1) // sections + (2 * sections - 2 - sec) // sections
    pl.semaphore_wait(barrier, 3 + len(group) + 4 * neighbours)

    low, high = pl.ds(0, half), pl.ds(half, half)
    w_low, w_high = pl.ds(0, w_half), pl.ds(w_half, w_half)
    og_r_low = copy(next(ids), og_ref.at[low], og_all.at[1, low], at_x(1))
    og_r_high = copy(next(ids), og_ref.at[high], og_all.at[1, high], at_x(1))
    og_l_high = copy(next(ids), og_ref.at[high], og_all.at[2, high], at_x(3))
    og_l_low = copy(next(ids), og_ref.at[low], og_all.at[2, low], at_x(3))
    og_fr = copy(next(ids), og_all.at[1, low], og_all.at[3, low], at_x(1))
    og_fl = copy(next(ids), og_all.at[2, high], og_all.at[3, high], at_x(3))
    w_u_low = copy(next(ids), w_ref.at[w_low], w_all.at[1, c, w_low], at_z(1, 0))
    w_u_high = copy(next(ids), w_ref.at[w_high], w_all.at[1, c, w_high], at_z(1, 0))
    w_d_high = copy(next(ids), w_ref.at[w_high], w_all.at[2, c, w_high], at_z(3, 0))
    w_d_low = copy(next(ids), w_ref.at[w_low], w_all.at[2, c, w_low], at_z(3, 0))
    w_fu = copy(next(ids), w_all.at[1, c, w_low], w_all.at[3, c, w_low], at_z(1, 0))
    w_fd = copy(next(ids), w_all.at[2, c, w_high], w_all.at[3, c, w_high], at_z(3, 0))
    li_sends = [
        copy(next(ids), li_ref.at[:, columns(lax.rem(x + AWAY[n], 4))], li_all.at[n], at_x(AWAY[n]))
        for n in (1, 2, 3)
    ]
    st_sends = [copy(next(ids), st_all.at[0], st_all.at[n], at_x(AWAY[n])) for n in (1, 2, 3)]
    own_sib = next(ids)
    w_sib = copy(own_sib, w_ref, w_all.at[0, c], at_z(0, 1))
    w_sib_in = copy(own_sib, w_ref, w_all.at[0, other], at_z(0, 1))

    for step in (og_r_low, og_l_high, w_u_low, w_d_high, og_r_high, og_l_low, w_u_high, w_d_low, w_sib):
        step.start()
    for step in li_sends:
        step.start()
    local = [
        pltpu.make_async_copy(og_ref, og_all.at[0], local_sem.at[0]),
        pltpu.make_async_copy(li_ref.at[:, own_columns], li_all.at[0], local_sem.at[1]),
        pltpu.make_async_copy(w_ref, w_all.at[0, c], local_sem.at[2]),
    ]
    for step in local:
        step.start()

    sib_sends, sib_waits = [w_sib], {}

    def to_sibling(slot, part_rows):
        ident = next(ids)
        place = w_all.at[slot, c, part_rows]
        send = copy(ident, place, place, at_z(0, 1))
        send.start()
        sib_sends.append(send)
        sib_waits.setdefault(slot, []).append(copy(ident, place, w_all.at[slot, other, part_rows], at_z(0, 1)))

    values = li_ref[...].astype(F32)
    mean = jnp.sum(values, axis=1, keepdims=True) / feats
    center = values - mean
    variance = jnp.sum(center * center, axis=1, keepdims=True) / feats
    st_all[0] = stats_to_rows(mean, lax.rsqrt(variance + 1e-06))
    for step in st_sends:
        step.start()
    gate_acc[...] = jnp.zeros_like(gate_acc)
    for step in local:
        step.wait()

    def scale_grad(n):
        gate = mod_ref[2, pl.ds(slot_x[n], 1), :]
        scaled[n] = (gate * og_all[n].astype(F32)).astype(BF16)

    def modulate(n):
        mean_n, inv_n = rows_to_stats(st_all[n])
        inv_all[n] = inv_n
        norm_n = (li_all[n].astype(F32) - mean_n) * inv_n
        normed[n] = norm_n
        scale = mod_ref[1, pl.ds(slot_x[n], 1), own_columns]
        shift = mod_ref[0, pl.ds(slot_x[n], 1), own_columns]
        mod_n = (norm_n * (1.0 + scale) + shift).astype(BF16)
        for j in range(4):
            modulated[j, n] = mod_n[:, j * chunk:(j + 1) * chunk]

    scale_grad(0)
    modulate(0)

    og_r_low.wait_recv()
    og_fr.start()
    og_l_high.wait_recv()
    og_fl.start()
    w_u_low.wait_recv()
    w_fu.start()
    to_sibling(1, w_low)
    w_d_high.wait_recv()
    w_fd.start()
    to_sibling(2, w_high)
    og_r_high.wait_recv()
    og_l_low.wait_recv()
    scale_grad(1)
    scale_grad(2)
    for n in (1, 2):
        li_sends[n - 1].wait_recv()
        st_sends[n - 1].wait_recv()
        modulate(n)
    w_u_high.wait_recv()
    to_sibling(1, w_high)
    w_d_low.wait_recv()
    to_sibling(2, w_low)
    w_sib_in.wait_recv()
    for slot in (1, 2):
        for step in sib_waits[slot]:
            step.wait_recv()

    tile = 512

    def chunk_of(slot):
        return lax.rem(z + jnp.where(slot == 1, 3, jnp.where(slot == 2, 1, jnp.where(slot == 3, 2, 0))), 4)

    def grad_product(slot, first, count):
        j = chunk_of(slot)
        left = scaled[first:first + count].reshape(count * rows, feats)
        right = w_all[slot].reshape(chunk, feats)
        product = lax.dot_general(left, right, (((1,), (1,)), ((), ())), preferred_element_type=F32)
        gm[j, first:first + count] = product.reshape(count, rows, chunk)

    def branch_product(slot, first, count):
        j = chunk_of(slot)

        def body(step, carry):
            cols = pl.ds(pl.multiple_of(step * tile, tile), tile)
            left = modulated[j, first:first + count].reshape(count * rows, chunk)
            right = w_all[slot, :, :, cols].reshape(chunk, tile)
            branch = jnp.dot(left, right, preferred_element_type=F32)
            weighed = branch.reshape(count, rows, tile) * og_all[first:first + count, :, cols].astype(F32)
            gate_acc[first:first + count, :, cols] += jnp.sum(
                weighed.reshape(count, rows // 8, 8, tile), axis=1
            )
            return carry

        lax.fori_loop(0, feats // tile, body, 0)

    def early(first, count):
        def body(slot, carry):
            grad_product(slot, first, count)
            branch_product(slot, first, count)
            return carry

        lax.fori_loop(0, 3, body, 0)

    early(0, 3)

    og_fr.wait_recv()
    og_fl.wait_recv()
    scale_grad(3)
    li_sends[2].wait_recv()
    st_sends[2].wait_recv()
    modulate(3)
    early(3, 1)

    w_fu.wait_recv()
    to_sibling(3, w_low)
    w_fd.wait_recv()
    to_sibling(3, w_high)
    for step in sib_waits[3]:
        step.wait_recv()
    grad_product(3, 0, 4)

    def joined(n):
        return jnp.concatenate([gm[j, n] for j in range(4)], axis=1)

    for n in range(4):
        scale = mod_ref[1, pl.ds(slot_x[n], 1), own_columns]
        grad_norm = joined(n) * (1.0 + scale)
        gn[n] = grad_norm
        sums[0, slot_x[n]] = stats_to_rows(
            jnp.sum(grad_norm, axis=1, keepdims=True),
            jnp.sum(grad_norm * normed[n], axis=1, keepdims=True),
        )
    sum_sends = [copy(next(ids), sums.at[0], sums.at[n], at_x(AWAY[n])) for n in (1, 2, 3)]
    for step in sum_sends:
        step.start()

    def place_rows(per_slot):
        row = lax.broadcasted_iota(jnp.int32, (SEQS, per_slot[0].shape[1]), 0)
        total = jnp.zeros(row.shape, F32)
        for n in range(4):
            total = total + jnp.where(row == slot_x[n], per_slot[n], 0.0)
        return total

    shifts, scales = [], []
    for n in range(4):
        grad_mod = joined(n)
        shifts.append(jnp.sum(grad_mod, axis=0, keepdims=True))
        scales.append(jnp.sum(grad_mod * normed[n], axis=0, keepdims=True))
    part[0] = place_rows(shifts)
    part[1] = place_rows(scales)

    for step in sum_sends:
        step.wait_recv()
    hand_ids = [next(ids) for n in range(4)]

    def hand(n):
        return copy(hand_ids[n], outgoing.at[n], out_ref.at[:, own_columns], at_section(-1, slot_x[n]))

    for n in range(4):
        rows_of = sums[0, slot_x[n]] + sums[1, slot_x[n]] + sums[2, slot_x[n]] + sums[3, slot_x[n]]
        first, second = rows_to_stats(rows_of)
        centered = gn[n] - first / feats
        grad_in = og_all[n, :, own_columns].astype(F32) + inv_all[n] * (centered - normed[n] * (second / feats))
        outgoing[n] = grad_in.astype(BF16)

        @pl.when(sec > 0)
        def _(n=n):
            hand(n).start()

    @pl.when(sec == sections - 1)
    def _():
        out_ref[...] = jnp.zeros_like(out_ref)

    branch_product(3, 0, 4)

    gate_buf[...] = place_rows([jnp.sum(gate_acc[n], axis=0, keepdims=True) for n in range(4)])
    gate_sends = [
        copy(next(ids), gate_buf.at[:, columns(lax.rem(x + AWAY[n], 4))], gate_rx.at[n - 1], at_x(AWAY[n]))
        for n in (1, 2, 3)
    ]
    for step in gate_sends:
        step.start()
    for step in gate_sends:
        step.wait_recv()
    part[2] = gate_buf[:, own_columns] + gate_rx[0] + gate_rx[1] + gate_rx[2]

    def owned(owner):
        return pl.ds(pl.multiple_of(owner * LANES, LANES), LANES)

    owns = z < owners // 2
    me = z * 2 + c
    rs_ids = [next(ids) for _ in group]
    ag_ids = [next(ids) for _ in group]

    def rs_copy(i):
        dz, dc = group[i]
        owner = lax.rem(z + dz, 4) * 2 + lax.rem(c + dc, 2)
        return copy(rs_ids[i], part.at[:, :, owned(owner)], rs.at[i], at_z(dz, dc))

    def gives(i):
        return lax.rem(z + group[i][0], 4) < owners // 2

    for i in range(len(group)):
        @pl.when(gives(i))
        def _(i=i):
            rs_copy(i).start()

    @pl.when(owns)
    def _():
        total = part[:, :, owned(me)]
        for i in range(len(group)):
            dz, dc = group[i]
            copy(rs_ids[i], rs.at[i], rs.at[i], at_z(dz, dc)).wait_recv()
        for i in range(len(group)):
            total = total + rs[i]
        full[0, me] = total
        for i in range(len(group)):
            dz, dc = group[i]
            copy(ag_ids[i], full.at[0, me], full.at[0, me], at_z(dz, dc)).start()

    for i in range(len(group)):
        dz, dc = group[i]
        from_z = lax.rem(z + 4 - dz, 4)
        source = from_z * 2 + lax.rem(c + dc, 2)

        @pl.when(from_z < owners // 2)
        def _(i=i, source=source, dz=dz, dc=dc):
            landed = full.at[0, source]
            copy(ag_ids[i], landed, landed, at_z(dz, dc)).wait_recv()

    full_sends = [copy(next(ids), full.at[0], full.at[n], at_x(AWAY[n])) for n in (1, 2, 3)]
    for step in full_sends:
        step.start()
    for step in full_sends:
        step.wait_recv()
    for n in range(4):
        for owner in range(owners):
            start = pl.multiple_of(slot_x[n] * block + owner * LANES, LANES)
            mg_ref[:, :, pl.ds(start, LANES)] = full[n, owner]

    for step in (
        og_r_low, og_r_high, og_l_high, og_l_low, og_fr, og_fl, w_u_low, w_u_high, w_d_high, w_d_low,
        w_fu, w_fd, *li_sends, *st_sends, *sib_sends, *sum_sends, *gate_sends, *full_sends,
    ):
        step.wait_send()
    for i in range(len(group)):
        @pl.when(gives(i))
        def _(i=i):
            rs_copy(i).wait_send()

    @pl.when(owns)
    def _():
        for i in range(len(group)):
            dz, dc = group[i]
            copy(ag_ids[i], full.at[0, me], full.at[0, me], at_z(dz, dc)).wait_send()

    @pl.when(sec > 0)
    def _():
        for n in range(4):
            hand(n).wait_send()

    @pl.when(sec < sections - 1)
    def _():
        for n in range(4):
            landed = out_ref.at[:, columns(lax.rem(x + 4 - OFF[n], 4))]
            copy(hand_ids[n], outgoing.at[n], landed, at_section(1, slot_x[n])).wait_recv()


def on_device(layer_input, out_grad, modulation, proj_weight):
    sections = lax.axis_size("section")
    rows, feats = layer_input.shape[1:]
    w_rows = proj_weight.shape[1]
    block, chunk = feats // 4, feats // 16
    owners = block // LANES
    vmem = pl.BlockSpec(memory_space=pltpu.VMEM)
    handoff, grads = pl.pallas_call(
        functools.partial(kernel, sections),
        out_shape=(
            jax.ShapeDtypeStruct((rows, feats), BF16),
            jax.ShapeDtypeStruct((3, SEQS, feats), F32),
        ),
        in_specs=[vmem] * 4,
        out_specs=(vmem, vmem),
        scratch_shapes=[
            pltpu.VMEM((4, rows, feats), BF16),
            pltpu.VMEM((4, rows, block), BF16),
            pltpu.VMEM((4, 2, w_rows, feats), BF16),
            pltpu.VMEM((4, 8, LANES), F32),
            pltpu.VMEM((4, rows, feats), BF16),
            pltpu.VMEM((4, rows, block), F32),
            pltpu.VMEM((4, rows, 1), F32),
            pltpu.VMEM((4, 4, rows, chunk), BF16),
            pltpu.VMEM((4, 4, rows, chunk), F32),
            pltpu.VMEM((4, rows, block), F32),
            pltpu.VMEM((4, rows, block), BF16),
            pltpu.VMEM((4, 8, feats), F32),
            pltpu.VMEM((4, 4, 8, LANES), F32),
            pltpu.VMEM((3, SEQS, block), F32),
            pltpu.VMEM((SEQS, feats), F32),
            pltpu.VMEM((3, SEQS, block), F32),
            pltpu.VMEM((7, 3, SEQS, LANES), F32),
            pltpu.VMEM((4, owners, 3, SEQS, LANES), F32),
            pltpu.SemaphoreType.DMA((COPIES,)),
            pltpu.SemaphoreType.DMA((COPIES,)),
            pltpu.SemaphoreType.DMA((3,)),
        ],
        compiler_params=pltpu.CompilerParams(
            collective_id=0, has_side_effects=True, vmem_limit_bytes=56 * 1024 * 1024
        ),
    )(layer_input[0], out_grad[0], jnp.transpose(modulation[0], (1, 0, 2)), proj_weight[0])
    return (handoff[None], jnp.transpose(grads, (1, 0, 2))[None])


def solution(mesh):
    in_specs = (
        P("section", "shard", None),
        P("section", "shard", None),
        P("section", None, None, None),
        P("section", "shard", None),
    )
    out_specs = (P("section", "shard", None), P("section", None, None, None))
    return jax.shard_map(
        on_device, mesh=mesh, in_specs=in_specs, out_specs=out_specs, check_vma=False
    )
```

```python
import functools

import jax
import jax.numpy as jnp
from jax import lax
from jax.experimental import pallas as pl
from jax.experimental.pallas import tpu as pltpu
from jax.sharding import PartitionSpec as P

MESH = pl.DeviceIdType.MESH
F32 = jnp.float32
BF16 = jnp.bfloat16

SEQS = 4
OFF = (0, 3, 1, 2)
AWAY = (0, 1, 3, 2)
LANES = 128
COPIES = 64


def stats_to_rows(first, second):
    lane = lax.broadcasted_iota(jnp.int32, (LANES, LANES), 1)
    square = jnp.where(lane == 0, first, jnp.where(lane == 1, second, 0.0))
    return jnp.transpose(square)[:8]


def rows_to_stats(rows):
    square = jnp.concatenate([rows, jnp.zeros((LANES - 8, LANES), F32)], axis=0)
    columns = jnp.transpose(square)
    return columns[:, 0:1], columns[:, 1:2]


def kernel(
    sections, li_ref, og_ref, mod_ref, w_ref, out_ref, mg_ref,
    li_own, og_all, li_all, w_all, st_all, scaled, normed, inv_all, modulated, gm, gn, outgoing,
    gate_acc, sums, part, part_rx, gate_buf, gate_rx, by_z, full, send_sem, recv_sem, local_sem,
):
    rows, feats = og_ref.shape
    block = feats // 4
    chunk = feats // 16
    w_rows = w_ref.shape[0]
    lot = block // 2
    half, w_half = rows // 2, w_rows // 2

    sec = lax.axis_index("section")
    shard = lax.axis_index("shard")
    x = shard // 8
    z = (shard % 8) // 2
    c = shard % 2
    other = 1 - c

    def at_x(k):
        return (sec, lax.rem(x + k, 4) * 8 + z * 2 + c)

    def at_z(dz, dc):
        return (sec, x * 8 + lax.rem(z + dz, 4) * 2 + lax.rem(c + dc, 2))

    def at_plane(k, dc):
        return (sec, lax.rem(x + k, 4) * 8 + z * 2 + lax.rem(c + dc, 2))

    def at_section(step, pos):
        return (sec + step, pos * 8 + z * 2 + c)

    def copy(ident, src, dst, device):
        return pltpu.make_async_remote_copy(
            src_ref=src, dst_ref=dst, send_sem=send_sem.at[ident], recv_sem=recv_sem.at[ident],
            device_id=device, device_id_type=MESH,
        )

    ids = iter(range(COPIES))
    slot_x = [lax.rem(x + OFF[n], 4) for n in range(4)]
    plane = [(k, dc) for k in range(4) for dc in range(2) if (k, dc) != (0, 0)]

    def columns(pos):
        return pl.ds(pl.multiple_of(pos * block, LANES), block)

    own_columns = columns(x)

    barrier = pltpu.get_barrier_semaphore()

    def greet(device):
        pl.semaphore_signal(barrier, inc=1, device_id=device, device_id_type=MESH)

    for k, dc in plane:
        greet(at_plane(k, dc))
    for dz in range(1, 4):
        greet(at_z(dz, 0))

    @pl.when(sec > 0)
    def _():
        for pos in range(4):
            greet(at_section(-1, pos))

    @pl.when(sec < sections - 1)
    def _():
        for pos in range(4):
            greet(at_section(1, pos))

    neighbours = (sec + sections - 1) // sections + (2 * sections - 2 - sec) // sections
    pl.semaphore_wait(barrier, 3 + len(plane) + 4 * neighbours)

    low, high = pl.ds(0, half), pl.ds(half, half)
    w_low, w_high = pl.ds(0, w_half), pl.ds(w_half, w_half)
    og_r_low = copy(next(ids), og_ref.at[low], og_all.at[1, low], at_x(1))
    og_r_high = copy(next(ids), og_ref.at[high], og_all.at[1, high], at_x(1))
    og_l_high = copy(next(ids), og_ref.at[high], og_all.at[2, high], at_x(3))
    og_l_low = copy(next(ids), og_ref.at[low], og_all.at[2, low], at_x(3))
    og_fr = copy(next(ids), og_all.at[1, low], og_all.at[3, low], at_x(1))
    og_fl = copy(next(ids), og_all.at[2, high], og_all.at[3, high], at_x(3))
    w_u_low = copy(next(ids), w_ref.at[w_low], w_all.at[1, c, w_low], at_z(1, 0))
    w_u_high = copy(next(ids), w_ref.at[w_high], w_all.at[1, c, w_high], at_z(1, 0))
    w_d_high = copy(next(ids), w_ref.at[w_high], w_all.at[2, c, w_high], at_z(3, 0))
    w_d_low = copy(next(ids), w_ref.at[w_low], w_all.at[2, c, w_low], at_z(3, 0))
    w_fu = copy(next(ids), w_all.at[1, c, w_low], w_all.at[3, c, w_low], at_z(1, 0))
    w_fd = copy(next(ids), w_all.at[2, c, w_high], w_all.at[3, c, w_high], at_z(3, 0))
    li_sends = [
        copy(next(ids), li_ref.at[:, columns(lax.rem(x + AWAY[n], 4))], li_all.at[n], at_x(AWAY[n]))
        for n in (1, 2, 3)
    ]
    st_sends = [copy(next(ids), st_all.at[0], st_all.at[n], at_x(AWAY[n])) for n in (1, 2, 3)]
    own_sib = next(ids)
    w_sib = copy(own_sib, w_ref, w_all.at[0, c], at_z(0, 1))
    w_sib_in = copy(own_sib, w_ref, w_all.at[0, other], at_z(0, 1))

    for step in (og_r_low, og_l_high, w_u_low, w_d_high, og_r_high, og_l_low, w_u_high, w_d_low, w_sib):
        step.start()
    for step in li_sends:
        step.start()
    local = [
        pltpu.make_async_copy(og_ref, og_all.at[0], local_sem.at[0]),
        pltpu.make_async_copy(li_ref, li_own, local_sem.at[1]),
        pltpu.make_async_copy(w_ref, w_all.at[0, c], local_sem.at[2]),
    ]
    for step in local:
        step.start()

    sib_sends, sib_waits = [w_sib], {}

    def to_sibling(slot, part_rows):
        ident = next(ids)
        place = w_all.at[slot, c, part_rows]
        send = copy(ident, place, place, at_z(0, 1))
        send.start()
        sib_sends.append(send)
        sib_waits.setdefault(slot, []).append(copy(ident, place, w_all.at[slot, other, part_rows], at_z(0, 1)))

    for step in local:
        step.wait()
    li_all[0] = li_own[:, own_columns]
    values = li_own[...].astype(F32)
    mean = jnp.sum(values, axis=1, keepdims=True) / feats
    center = values - mean
    variance = jnp.sum(center * center, axis=1, keepdims=True) / feats
    st_all[0] = stats_to_rows(mean, lax.rsqrt(variance + 1e-06))
    for step in st_sends:
        step.start()
    gate_acc[...] = jnp.zeros_like(gate_acc)

    def scale_grad(n):
        gate = mod_ref[2, pl.ds(slot_x[n], 1), :]
        scaled[n] = (gate * og_all[n].astype(F32)).astype(BF16)

    def modulate(n):
        mean_n, inv_n = rows_to_stats(st_all[n])
        inv_all[n] = inv_n
        norm_n = (li_all[n].astype(F32) - mean_n) * inv_n
        normed[n] = norm_n
        scale = mod_ref[1, pl.ds(slot_x[n], 1), own_columns]
        shift = mod_ref[0, pl.ds(slot_x[n], 1), own_columns]
        mod_n = (norm_n * (1.0 + scale) + shift).astype(BF16)
        for j in range(4):
            modulated[j, n] = mod_n[:, j * chunk:(j + 1) * chunk]

    scale_grad(0)
    modulate(0)

    og_r_low.wait_recv()
    og_fr.start()
    og_l_high.wait_recv()
    og_fl.start()
    w_u_low.wait_recv()
    w_fu.start()
    to_sibling(1, w_low)
    w_d_high.wait_recv()
    w_fd.start()
    to_sibling(2, w_high)
    og_r_high.wait_recv()
    og_l_low.wait_recv()
    scale_grad(1)
    scale_grad(2)
    for n in (1, 2):
        li_sends[n - 1].wait_recv()
        st_sends[n - 1].wait_recv()
        modulate(n)
    tile = 512

    def chunk_of(slot):
        return lax.rem(z + OFF[slot], 4)

    def grad_product(slot, first, count):
        left = scaled[first:first + count].reshape(count * rows, feats)
        right = w_all[slot].reshape(chunk, feats)
        product = lax.dot_general(left, right, (((1,), (1,)), ((), ())), preferred_element_type=F32)
        gm[chunk_of(slot), first:first + count] = product.reshape(count, rows, chunk)

    def branch_product(slots, first, count):
        def body(step, carry):
            cols = pl.ds(pl.multiple_of(step * tile, tile), tile)
            branch = None
            for slot in slots:
                left = modulated[chunk_of(slot), first:first + count].reshape(count * rows, chunk)
                right = w_all[slot, :, :, cols].reshape(chunk, tile)
                term = jnp.dot(left, right, preferred_element_type=F32)
                branch = term if branch is None else branch + term
            weighed = branch.reshape(count, rows, tile) * og_all[first:first + count, :, cols].astype(F32)
            gate_acc[first:first + count, :, cols] += jnp.sum(
                weighed.reshape(count, rows // 8, 8, tile), axis=1
            )
            return carry

        lax.fori_loop(0, feats // tile, body, 0)

    w_sib_in.wait_recv()
    grad_product(0, 0, 3)
    branch_product((0,), 0, 3)

    w_u_high.wait_recv()
    to_sibling(1, w_high)
    w_d_low.wait_recv()
    to_sibling(2, w_low)
    for slot in (1, 2):
        for step in sib_waits[slot]:
            step.wait_recv()
        grad_product(slot, 0, 3)

    og_fr.wait_recv()
    og_fl.wait_recv()
    scale_grad(3)
    li_sends[2].wait_recv()
    st_sends[2].wait_recv()
    modulate(3)
    for slot in (0, 1, 2):
        grad_product(slot, 3, 1)
    branch_product((1, 2), 0, 3)
    branch_product((0, 1, 2), 3, 1)

    w_fu.wait_recv()
    to_sibling(3, w_low)
    w_fd.wait_recv()
    to_sibling(3, w_high)
    for step in sib_waits[3]:
        step.wait_recv()
    grad_product(3, 0, 4)

    def joined(n):
        return jnp.concatenate([gm[j, n] for j in range(4)], axis=1)

    for n in range(4):
        scale = mod_ref[1, pl.ds(slot_x[n], 1), own_columns]
        grad_norm = joined(n) * (1.0 + scale)
        gn[n] = grad_norm
        sums[0, slot_x[n]] = stats_to_rows(
            jnp.sum(grad_norm, axis=1, keepdims=True),
            jnp.sum(grad_norm * normed[n], axis=1, keepdims=True),
        )
    sum_sends = [copy(next(ids), sums.at[0], sums.at[n], at_x(AWAY[n])) for n in (1, 2, 3)]
    for step in sum_sends:
        step.start()

    def place_rows(per_slot):
        row = lax.broadcasted_iota(jnp.int32, (SEQS, per_slot[0].shape[1]), 0)
        total = jnp.zeros(row.shape, F32)
        for n in range(4):
            total = total + jnp.where(row == slot_x[n], per_slot[n], 0.0)
        return total

    branch_product((3,), 0, 4)
    gate_buf[...] = place_rows([jnp.sum(gate_acc[n], axis=0, keepdims=True) for n in range(4)])

    def lot_of(pos, core):
        return pl.ds(pl.multiple_of(pos * block + core * lot, LANES), lot)

    gate_sends = [
        copy(
            next(ids), gate_buf.at[:, lot_of(lax.rem(x + k, 4), lax.rem(c + dc, 2))], gate_rx.at[i],
            at_plane(k, dc),
        )
        for i, (k, dc) in enumerate(plane)
    ]
    for step in gate_sends:
        step.start()

    for step in sum_sends:
        step.wait_recv()
    hand_ids = [next(ids) for n in range(4)]

    def hand(n):
        return copy(hand_ids[n], outgoing.at[n], out_ref.at[:, own_columns], at_section(-1, slot_x[n]))

    for n in range(4):
        rows_of = sums[0, slot_x[n]] + sums[1, slot_x[n]] + sums[2, slot_x[n]] + sums[3, slot_x[n]]
        first, second = rows_to_stats(rows_of)
        centered = gn[n] - first / feats
        grad_in = og_all[n, :, own_columns].astype(F32) + inv_all[n] * (centered - normed[n] * (second / feats))
        outgoing[n] = grad_in.astype(BF16)

        @pl.when(sec > 0)
        def _(n=n):
            hand(n).start()

    zero_copy = pltpu.make_async_copy(scaled.at[0], out_ref, local_sem.at[3])

    @pl.when(sec == sections - 1)
    def _():
        scaled[0] = jnp.zeros_like(scaled[0])
        zero_copy.start()

    shifts, scales = [], []
    for n in range(4):
        grad_mod = joined(n)
        shifts.append(jnp.sum(grad_mod, axis=0, keepdims=True))
        scales.append(jnp.sum(grad_mod * normed[n], axis=0, keepdims=True))
    part[0] = place_rows(shifts)
    part[1] = place_rows(scales)

    part_send = copy(next(ids), part.at[:, :, lot_of(0, other)], part_rx, at_z(0, 1))
    part_send.start()
    for step in gate_sends:
        step.wait_recv()
    gate = gate_buf[:, lot_of(x, c)]
    for i in range(len(plane)):
        gate = gate + gate_rx[i]
    by_z[z, 2] = gate
    part_send.wait_recv()
    by_z[z, 0:2] = part[:, :, lot_of(0, c)] + part_rx[...]
    z_ids = [next(ids) for _ in range(3)]
    z_sends = []
    for i in range(3):
        held = by_z.at[lax.rem(z + 4 - i, 4)]
        step = copy(z_ids[i], held, held, at_z(1, 0))
        step.start()
        z_sends.append(step)
        landed = by_z.at[lax.rem(z + 3 - i, 4)]
        copy(z_ids[i], landed, landed, at_z(1, 0)).wait_recv()
    full[x, c] = by_z[0] + by_z[1] + by_z[2] + by_z[3]
    full_ids = [next(ids) for _ in plane]
    full_sends = [
        copy(full_ids[i], full.at[x, c], full.at[x, c], at_plane(k, dc)) for i, (k, dc) in enumerate(plane)
    ]
    for step in full_sends:
        step.start()
    for i, (k, dc) in enumerate(plane):
        landed = full.at[lax.rem(x + 4 - k, 4), lax.rem(c + dc, 2)]
        copy(full_ids[i], landed, landed, at_plane(k, dc)).wait_recv()
    for pos in range(4):
        for core in range(2):
            start = pos * block + core * lot
            mg_ref[:, :, start:start + lot] = full[pos, core]

    for step in (
        og_r_low, og_r_high, og_l_high, og_l_low, og_fr, og_fl, w_u_low, w_u_high, w_d_high, w_d_low,
        w_fu, w_fd, *li_sends, *st_sends, *sib_sends, *sum_sends, *gate_sends, part_send, *z_sends, *full_sends,
    ):
        step.wait_send()
    @pl.when(sec > 0)
    def _():
        for n in range(4):
            hand(n).wait_send()

    @pl.when(sec < sections - 1)
    def _():
        for n in range(4):
            landed = out_ref.at[:, columns(lax.rem(x + 4 - OFF[n], 4))]
            copy(hand_ids[n], outgoing.at[n], landed, at_section(1, slot_x[n])).wait_recv()

    @pl.when(sec == sections - 1)
    def _():
        zero_copy.wait()


def on_device(layer_input, out_grad, modulation, proj_weight):
    sections = lax.axis_size("section")
    rows, feats = layer_input.shape[1:]
    w_rows = proj_weight.shape[1]
    block, chunk = feats // 4, feats // 16
    lot = block // 2
    vmem = pl.BlockSpec(memory_space=pltpu.VMEM)
    anywhere = pl.BlockSpec(memory_space=pl.ANY)
    handoff, grads = pl.pallas_call(
        functools.partial(kernel, sections),
        out_shape=(
            jax.ShapeDtypeStruct((rows, feats), BF16),
            jax.ShapeDtypeStruct((3, SEQS, feats), F32),
        ),
        in_specs=[anywhere, anywhere, vmem, anywhere],
        out_specs=(anywhere, vmem),
        scratch_shapes=[
            pltpu.VMEM((rows, feats), BF16),
            pltpu.VMEM((4, rows, feats), BF16),
            pltpu.VMEM((4, rows, block), BF16),
            pltpu.VMEM((4, 2, w_rows, feats), BF16),
            pltpu.VMEM((4, 8, LANES), F32),
            pltpu.VMEM((4, rows, feats), BF16),
            pltpu.VMEM((4, rows, block), F32),
            pltpu.VMEM((4, rows, 1), F32),
            pltpu.VMEM((4, 4, rows, chunk), BF16),
            pltpu.VMEM((4, 4, rows, chunk), F32),
            pltpu.VMEM((4, rows, block), F32),
            pltpu.VMEM((4, rows, block), BF16),
            pltpu.VMEM((4, 8, feats), F32),
            pltpu.VMEM((4, 4, 8, LANES), F32),
            pltpu.VMEM((2, SEQS, block), F32),
            pltpu.VMEM((2, SEQS, lot), F32),
            pltpu.VMEM((SEQS, feats), F32),
            pltpu.VMEM((7, SEQS, lot), F32),
            pltpu.VMEM((4, 3, SEQS, lot), F32),
            pltpu.VMEM((4, 2, 3, SEQS, lot), F32),
            pltpu.SemaphoreType.DMA((COPIES,)),
            pltpu.SemaphoreType.DMA((COPIES,)),
            pltpu.SemaphoreType.DMA((4,)),
        ],
        compiler_params=pltpu.CompilerParams(
            collective_id=0, has_side_effects=True, vmem_limit_bytes=56 * 1024 * 1024
        ),
    )(layer_input[0], out_grad[0], jnp.transpose(modulation[0], (1, 0, 2)), proj_weight[0])
    return (handoff[None], jnp.transpose(grads, (1, 0, 2))[None])


def solution(mesh):
    in_specs = (
        P("section", "shard", None),
        P("section", "shard", None),
        P("section", None, None, None),
        P("section", "shard", None),
    )
    out_specs = (P("section", "shard", None), P("section", None, None, None))
    return jax.shard_map(
        on_device, mesh=mesh, in_specs=in_specs, out_specs=out_specs, check_vma=False
    )
```

```python
import functools

import jax
import jax.numpy as jnp
from jax import lax
from jax.experimental import pallas as pl
from jax.experimental.pallas import tpu as pltpu
from jax.sharding import PartitionSpec as P

MESH = pl.DeviceIdType.MESH
F32 = jnp.float32
BF16 = jnp.bfloat16

SEQS = 4
OFF = (0, 3, 1, 2)
AWAY = (0, 1, 3, 2)
LANES = 128
COPIES = 96


def stats_to_rows(first, second):
    lane = lax.broadcasted_iota(jnp.int32, (LANES, LANES), 1)
    square = jnp.where(lane == 0, first, jnp.where(lane == 1, second, 0.0))
    return jnp.transpose(square)[:8]


def rows_to_stats(rows):
    square = jnp.concatenate([rows, jnp.zeros((LANES - 8, LANES), F32)], axis=0)
    columns = jnp.transpose(square)
    return columns[:, 0:1], columns[:, 1:2]


def kernel(
    sections, li_ref, og_ref, mod_ref, w_ref, out_ref, mg_ref,
    li_own, og_all, li_all, w_all, st_all, scaled, normed, inv_all, modulated, gm, norm_by, first_sum, second_sum, outgoing,
    gate_acc, sums, part, part_rx, gate_buf, gate_rx, by_z, full, factor, chunk_tx, chunk_rx,
    next_li, next_og, mean_tx, mean_rx, ready, relay, send_sem, recv_sem, local_sem,
):
    rows, feats = og_ref.shape
    block = feats // 4
    chunk = feats // 16
    w_rows = w_ref.shape[0]
    lot = block // 2
    half, w_half = rows // 2, w_rows // 2

    sec = lax.axis_index("section")
    shard = lax.axis_index("shard")
    x = shard // 8
    z = (shard % 8) // 2
    c = shard % 2
    other = 1 - c

    def at_x(k):
        return (sec, lax.rem(x + k, 4) * 8 + z * 2 + c)

    def at_z(dz, dc):
        return (sec, x * 8 + lax.rem(z + dz, 4) * 2 + lax.rem(c + dc, 2))

    def at_plane(k, dc):
        return (sec, lax.rem(x + k, 4) * 8 + z * 2 + lax.rem(c + dc, 2))

    def at_section(step, pos):
        return (sec + step, pos * 8 + z * 2 + c)

    def copy(ident, src, dst, device):
        return pltpu.make_async_remote_copy(
            src_ref=src, dst_ref=dst, send_sem=send_sem.at[ident], recv_sem=recv_sem.at[ident],
            device_id=device, device_id_type=MESH,
        )

    corner = sections // 2
    streams = jnp.logical_and(sec > 0, sec != corner)
    hears = jnp.logical_and(sec < sections - 1, sec != corner - 1)

    ids = iter(range(COPIES))
    slot_x = [lax.rem(x + OFF[n], 4) for n in range(4)]
    plane = [(k, dc) for k in range(4) for dc in range(2) if (k, dc) != (0, 0)]

    def columns(pos):
        return pl.ds(pl.multiple_of(pos * block, LANES), block)

    own_columns = columns(x)

    barrier = pltpu.get_barrier_semaphore()

    def greet(device):
        pl.semaphore_signal(barrier, inc=1, device_id=device, device_id_type=MESH)

    for k, dc in plane:
        greet(at_plane(k, dc))
    for dz in range(1, 4):
        greet(at_z(dz, 0))

    @pl.when(sec > 0)
    def _():
        for pos in range(4):
            greet(at_section(-1, pos))

    @pl.when(sec < sections - 1)
    def _():
        for pos in range(4):
            greet(at_section(1, pos))

    @pl.when(sec == corner)
    def _():
        for pos in range(4):
            greet(at_section(-corner, pos))

    @pl.when(sec == 0)
    def _():
        for pos in range(4):
            greet(at_section(corner, pos))
        greet(at_section(corner - 1, x))

    @pl.when(sec == corner - 1)
    def _():
        greet(at_section(1 - corner, x))

    def one_if(test):
        return jnp.where(test, 1, 0)

    extra = 4 * one_if(sec == corner) + 5 * one_if(sec == 0) + one_if(sec == corner - 1)
    neighbours = (sec + sections - 1) // sections + (2 * sections - 2 - sec) // sections
    pl.semaphore_wait(barrier, 3 + len(plane) + 4 * neighbours + extra)

    low, high = pl.ds(0, half), pl.ds(half, half)
    w_low, w_high = pl.ds(0, w_half), pl.ds(w_half, w_half)
    og_r_low = copy(next(ids), og_ref.at[low], og_all.at[1, low], at_x(1))
    og_r_high = copy(next(ids), og_ref.at[high], og_all.at[1, high], at_x(1))
    og_l_high = copy(next(ids), og_ref.at[high], og_all.at[2, high], at_x(3))
    og_l_low = copy(next(ids), og_ref.at[low], og_all.at[2, low], at_x(3))
    og_fr = copy(next(ids), og_all.at[1, low], og_all.at[3, low], at_x(1))
    og_fl = copy(next(ids), og_all.at[2, high], og_all.at[3, high], at_x(3))
    w_u_low = copy(next(ids), w_ref.at[w_low], w_all.at[1, c, w_low], at_z(1, 0))
    w_u_high = copy(next(ids), w_ref.at[w_high], w_all.at[1, c, w_high], at_z(1, 0))
    w_d_high = copy(next(ids), w_ref.at[w_high], w_all.at[2, c, w_high], at_z(3, 0))
    w_d_low = copy(next(ids), w_ref.at[w_low], w_all.at[2, c, w_low], at_z(3, 0))
    w_fu = copy(next(ids), w_all.at[1, c, w_low], w_all.at[3, c, w_low], at_z(1, 0))
    w_fd = copy(next(ids), w_all.at[2, c, w_high], w_all.at[3, c, w_high], at_z(3, 0))
    li_sends = [
        copy(next(ids), li_ref.at[:, columns(lax.rem(x + AWAY[n], 4))], li_all.at[n], at_x(AWAY[n]))
        for n in (1, 2, 3)
    ]
    st_sends = [copy(next(ids), st_all.at[0], st_all.at[n], at_x(AWAY[n])) for n in (1, 2, 3)]
    own_sib = next(ids)
    w_sib = copy(own_sib, w_ref, w_all.at[0, c], at_z(0, 1))
    w_sib_in = copy(own_sib, w_ref, w_all.at[0, other], at_z(0, 1))

    for step in (og_r_low, og_l_high, w_u_low, w_d_high, og_r_high, og_l_low, w_u_high, w_d_low, w_sib):
        step.start()
    for step in li_sends:
        step.start()
    og_next = copy(next(ids), og_ref, next_og, at_section(-1, x))
    li_next = copy(next(ids), li_ref, next_li, at_section(-1, x))

    @pl.when(streams)
    def _():
        li_next.start()
        og_next.start()

    local = [
        pltpu.make_async_copy(og_ref, og_all.at[0], local_sem.at[0]),
        pltpu.make_async_copy(li_ref, li_own, local_sem.at[1]),
        pltpu.make_async_copy(w_ref, w_all.at[0, c], local_sem.at[2]),
    ]
    for step in local:
        step.start()

    sib_sends, sib_waits = [w_sib], {}

    def to_sibling(slot, part_rows):
        ident = next(ids)
        place = w_all.at[slot, c, part_rows]
        send = copy(ident, place, place, at_z(0, 1))
        send.start()
        sib_sends.append(send)
        sib_waits.setdefault(slot, []).append(copy(ident, place, w_all.at[slot, other, part_rows], at_z(0, 1)))

    for step in local:
        step.wait()
    li_all[0] = li_own[:, own_columns]
    values = li_own[...].astype(F32)
    mean = jnp.sum(values, axis=1, keepdims=True) / feats
    center = values - mean
    variance = jnp.sum(center * center, axis=1, keepdims=True) / feats
    st_all[0] = stats_to_rows(mean, lax.rsqrt(variance + 1e-06))
    for step in st_sends:
        step.start()
    gate_acc[...] = jnp.zeros_like(gate_acc)

    def scale_grad(n):
        gate = mod_ref[2, pl.ds(slot_x[n], 1), :]
        scaled[n] = (gate * og_all[n].astype(F32)).astype(BF16)

    def modulate(n):
        mean_n, inv_n = rows_to_stats(st_all[n])
        inv_all[n] = inv_n
        norm_n = (li_all[n].astype(F32) - mean_n) * inv_n
        normed[n] = norm_n
        scale = mod_ref[1, pl.ds(slot_x[n], 1), own_columns]
        shift = mod_ref[0, pl.ds(slot_x[n], 1), own_columns]
        mod_n = (norm_n * (1.0 + scale) + shift).astype(BF16)
        for j in range(4):
            modulated[j, n] = mod_n[:, j * chunk:(j + 1) * chunk]
            factor[j, n] = 1.0 + scale[:, j * chunk:(j + 1) * chunk]
            norm_by[j, n] = norm_n[:, j * chunk:(j + 1) * chunk]

    scale_grad(0)
    modulate(0)

    og_r_low.wait_recv()
    og_fr.start()
    og_l_high.wait_recv()
    og_fl.start()
    w_u_low.wait_recv()
    w_fu.start()
    to_sibling(1, w_low)
    w_d_high.wait_recv()
    w_fd.start()
    to_sibling(2, w_high)
    og_r_high.wait_recv()
    og_l_low.wait_recv()
    scale_grad(1)
    scale_grad(2)
    for n in (1, 2):
        li_sends[n - 1].wait_recv()
        st_sends[n - 1].wait_recv()
        modulate(n)
    tile = 512

    def chunk_of(slot):
        return lax.rem(z + OFF[slot], 4)

    sum_sends = [copy(next(ids), sums.at[0], sums.at[n], at_x(AWAY[n])) for n in (1, 2, 3)]
    chunk_ids = [[next(ids) for n in range(4)] for slot in range(4)]

    def chunk_copy(slot, n):
        j = chunk_of(slot)
        return copy(chunk_ids[slot][n], chunk_tx.at[n, j], chunk_rx.at[n, j], at_section(-1, slot_x[n]))

    def grad_product(slot, first, count):
        left = scaled[first:first + count].reshape(count * rows, feats)
        right = w_all[slot].reshape(chunk, feats)
        product = lax.dot_general(left, right, (((1,), (1,)), ((), ())), preferred_element_type=F32)
        gm[chunk_of(slot), first:first + count] = product.reshape(count, rows, chunk)
        for n in range(first, first + count):
            grad_norm = gm[chunk_of(slot), n] * factor[chunk_of(slot), n]
            one = jnp.sum(grad_norm, axis=1, keepdims=True)
            two = jnp.sum(grad_norm * norm_by[chunk_of(slot), n], axis=1, keepdims=True)
            if slot == 3:
                sums[0, slot_x[n]] = stats_to_rows(first_sum[n] + one, second_sum[n] + two)
            elif slot == 0:
                first_sum[n] = one
                second_sum[n] = two
            else:
                first_sum[n] += one
                second_sum[n] += two
        if slot == 3:
            for step in sum_sends:
                step.start()

        @pl.when(streams)
        def _():
            for n in range(first, first + count):
                term = inv_all[n] * (gm[chunk_of(slot), n] * factor[chunk_of(slot), n])
                chunk_tx[n, chunk_of(slot)] = term.astype(BF16)
                chunk_copy(slot, n).start()

    def branch_product(slots, first, count):
        def body(step, carry):
            cols = pl.ds(pl.multiple_of(step * tile, tile), tile)
            branch = None
            for slot in slots:
                left = modulated[chunk_of(slot), first:first + count].reshape(count * rows, chunk)
                right = w_all[slot, :, :, cols].reshape(chunk, tile)
                term = jnp.dot(left, right, preferred_element_type=F32)
                branch = term if branch is None else branch + term
            weighed = branch.reshape(count, rows, tile) * og_all[first:first + count, :, cols].astype(F32)
            gate_acc[first:first + count, :, cols] += jnp.sum(
                weighed.reshape(count, rows // 8, 8, tile), axis=1
            )
            return carry

        lax.fori_loop(0, feats // tile, body, 0)

    w_sib_in.wait_recv()
    grad_product(0, 0, 3)
    branch_product((0,), 0, 3)

    w_u_high.wait_recv()
    to_sibling(1, w_high)
    w_d_low.wait_recv()
    to_sibling(2, w_low)
    for slot in (1, 2):
        for step in sib_waits[slot]:
            step.wait_recv()
        grad_product(slot, 0, 3)

    og_fr.wait_recv()
    og_fl.wait_recv()
    scale_grad(3)
    li_sends[2].wait_recv()
    st_sends[2].wait_recv()
    modulate(3)
    for slot in (0, 1, 2):
        grad_product(slot, 3, 1)
    branch_product((1, 2), 0, 3)
    branch_product((0, 1, 2), 3, 1)

    w_fu.wait_recv()
    to_sibling(3, w_low)
    w_fd.wait_recv()
    to_sibling(3, w_high)
    for step in sib_waits[3]:
        step.wait_recv()
    grad_product(3, 0, 4)

    def joined(n):
        return jnp.concatenate([gm[j, n] for j in range(4)], axis=1)

    def place_rows(per_slot):
        row = lax.broadcasted_iota(jnp.int32, (SEQS, per_slot[0].shape[1]), 0)
        total = jnp.zeros(row.shape, F32)
        for n in range(4):
            total = total + jnp.where(row == slot_x[n], per_slot[n], 0.0)
        return total

    branch_product((3,), 0, 4)
    def lot_of(pos, core):
        return pl.ds(pl.multiple_of(pos * block + core * lot, LANES), lot)

    gate_sends = [
        copy(
            next(ids), gate_buf.at[:, lot_of(lax.rem(x + k, 4), lax.rem(c + dc, 2))], gate_rx.at[i],
            at_plane(k, dc),
        )
        for i, (k, dc) in enumerate(plane)
    ]
    def send_gates():
        gate_buf[...] = place_rows([jnp.sum(gate_acc[n], axis=0, keepdims=True) for n in range(4)])
        for step in gate_sends:
            step.start()

    pl.when(sec != corner)(send_gates)

    for step in sum_sends:
        step.wait_recv()
    def row_means(n):
        rows_of = sums[0, slot_x[n]] + sums[1, slot_x[n]] + sums[2, slot_x[n]] + sums[3, slot_x[n]]
        return rows_of

    mean_tx[...] = row_means(0)
    mean_send = copy(next(ids), mean_tx, mean_rx, at_section(-1, x))

    @pl.when(streams)
    def _():
        mean_send.start()

    hand_ids = [next(ids) for n in range(4)]

    def hand(n):
        return copy(hand_ids[n], outgoing.at[n, straight], out_ref.at[straight, own_columns], at_section(-1, slot_x[n]))

    via_ids = [next(ids) for n in range(4)]
    relay_ids = [next(ids) for n in range(4)]
    straight, around = pl.ds(0, rows - relay.shape[1]), pl.ds(rows - relay.shape[1], relay.shape[1])

    def via(n):
        return copy(via_ids[n], outgoing.at[n, around], relay.at[n], at_section(-corner, slot_x[n]))

    def from_columns(n):
        return columns(lax.rem(x + 4 - OFF[n], 4))

    def relayed(n):
        return copy(relay_ids[n], relay.at[n], out_ref.at[around, from_columns(n)], at_section(corner - 1, x))

    def pass_on(*which):
        @pl.when(sec == 0)
        def _():
            for n in which:
                copy(via_ids[n], relay.at[n], relay.at[n], at_section(corner, slot_x[n])).wait_recv()
                relayed(n).start()

    @pl.when(sec == corner)
    def _():
        for n in range(4):
            first, second = rows_to_stats(row_means(n))
            scale = mod_ref[1, pl.ds(slot_x[n], 1), own_columns]
            centered = joined(n) * (1.0 + scale) - first / feats
            grad_in = og_all[n, :, own_columns].astype(F32) + inv_all[n] * (
                centered - normed[n] * (second / feats)
            )
            outgoing[n] = grad_in.astype(BF16)
            via(n).start()
            hand(n).start()

    pl.when(sec == corner)(send_gates)

    zero_copy = pltpu.make_async_copy(scaled.at[0], out_ref, local_sem.at[3])

    @pl.when(sec == sections - 1)
    def _():
        scaled[0] = jnp.zeros_like(scaled[0])
        zero_copy.start()

    shifts, scales = [], []
    for n in range(4):
        grad_mod = joined(n)
        shifts.append(jnp.sum(grad_mod, axis=0, keepdims=True))
        scales.append(jnp.sum(grad_mod * normed[n], axis=0, keepdims=True))
    part[0] = place_rows(shifts)
    part[1] = place_rows(scales)

    part_send = copy(next(ids), part.at[:, :, lot_of(0, other)], part_rx, at_z(0, 1))
    part_send.start()
    for step in gate_sends:
        step.wait_recv()
    gate = gate_buf[:, lot_of(x, c)]
    for i in range(len(plane)):
        gate = gate + gate_rx[i]
    by_z[z, 2] = gate
    part_send.wait_recv()
    by_z[z, 0:2] = part[:, :, lot_of(0, c)] + part_rx[...]
    z_ids = [next(ids) for _ in range(6)]
    edge_plane = lax.rem(sec, corner) == corner - 1

    def round_z(i):
        held = by_z.at[lax.rem(z + 4 - i, 4)]
        return copy(z_ids[i], held, held, at_z(1, 0))

    def across_z(i):
        return copy(z_ids[3 + i], by_z.at[z], by_z.at[z], at_z(i + 1, 0))

    @pl.when(edge_plane)
    def _():
        for i in range(3):
            round_z(i).start()
            landed = by_z.at[lax.rem(z + 3 - i, 4)]
            copy(z_ids[i], landed, landed, at_z(1, 0)).wait_recv()

    @pl.when(jnp.logical_not(edge_plane))
    def _():
        for i in range(3):
            across_z(i).start()
        pass_on(0)
        for i in range(3):
            landed = by_z.at[lax.rem(z + 3 - i, 4)]
            copy(z_ids[3 + i], landed, landed, at_z(i + 1, 0)).wait_recv()

    full[x, c] = by_z[0] + by_z[1] + by_z[2] + by_z[3]
    full_ids = [next(ids) for _ in plane]
    full_sends = [
        copy(full_ids[i], full.at[x, c], full.at[x, c], at_plane(k, dc)) for i, (k, dc) in enumerate(plane)
    ]
    for step in full_sends:
        step.start()
    pass_on(1, 2)

    def finished(n):
        return pltpu.make_async_copy(ready.at[n], out_ref.at[:, from_columns(n)], local_sem.at[4 + n])

    @pl.when(hears)
    def _():
        li_next.wait_recv()
        later = next_li[...].astype(F32)
        later_mean = jnp.sum(later, axis=1, keepdims=True) / feats
        later_center = later - later_mean
        later_inv = lax.rsqrt(jnp.sum(later_center * later_center, axis=1, keepdims=True) / feats + 1e-06)
        og_next.wait_recv()
        mean_send.wait_recv()
        first, second = rows_to_stats(mean_rx[...])
        for n in range(4):
            for slot in range(4):
                chunk_copy(slot, n).wait_recv()
            cols = from_columns(n)
            term = jnp.concatenate([chunk_rx[n, j].astype(F32) for j in range(4)], axis=1)
            norm_n = (next_li[:, cols].astype(F32) - later_mean) * later_inv
            taken = later_inv * (first / feats + norm_n * (second / feats))
            ready[n] = (next_og[:, cols].astype(F32) + (term - taken)).astype(BF16)
            finished(n).start()

    pass_on(3)
    for i, (k, dc) in enumerate(plane):
        landed = full.at[lax.rem(x + 4 - k, 4), lax.rem(c + dc, 2)]
        copy(full_ids[i], landed, landed, at_plane(k, dc)).wait_recv()
    for pos in range(4):
        for core in range(2):
            start = pos * block + core * lot
            mg_ref[:, :, start:start + lot] = full[pos, core]

    for step in (
        og_r_low, og_r_high, og_l_high, og_l_low, og_fr, og_fl, w_u_low, w_u_high, w_d_high, w_d_low,
        w_fu, w_fd, *li_sends, *st_sends, *sib_sends, *sum_sends, *gate_sends, part_send, *full_sends,
    ):
        step.wait_send()
    @pl.when(edge_plane)
    def _():
        for i in range(3):
            round_z(i).wait_send()

    @pl.when(jnp.logical_not(edge_plane))
    def _():
        for i in range(3):
            across_z(i).wait_send()

    @pl.when(streams)
    def _():
        og_next.wait_send()
        li_next.wait_send()
        mean_send.wait_send()
        for slot in range(4):
            for n in range(4):
                chunk_copy(slot, n).wait_send()

    @pl.when(hears)
    def _():
        for n in range(4):
            finished(n).wait()

    @pl.when(sec == corner)
    def _():
        for n in range(4):
            hand(n).wait_send()
            via(n).wait_send()

    @pl.when(sec == 0)
    def _():
        for n in range(4):
            relayed(n).wait_send()

    @pl.when(sec == corner - 1)
    def _():
        for n in range(4):
            landed = out_ref.at[straight, from_columns(n)]
            copy(hand_ids[n], outgoing.at[n, straight], landed, at_section(1, slot_x[n])).wait_recv()
            landed = out_ref.at[around, from_columns(n)]
            copy(relay_ids[n], relay.at[n], landed, at_section(1 - corner, x)).wait_recv()

    @pl.when(sec == sections - 1)
    def _():
        zero_copy.wait()


def on_device(layer_input, out_grad, modulation, proj_weight):
    sections = lax.axis_size("section")
    rows, feats = layer_input.shape[1:]
    w_rows = proj_weight.shape[1]
    block, chunk = feats // 4, feats // 16
    lot = block // 2
    vmem = pl.BlockSpec(memory_space=pltpu.VMEM)
    anywhere = pl.BlockSpec(memory_space=pl.ANY)
    handoff, grads = pl.pallas_call(
        functools.partial(kernel, sections),
        out_shape=(
            jax.ShapeDtypeStruct((rows, feats), BF16),
            jax.ShapeDtypeStruct((3, SEQS, feats), F32),
        ),
        in_specs=[anywhere, anywhere, vmem, anywhere],
        out_specs=(anywhere, vmem),
        scratch_shapes=[
            pltpu.VMEM((rows, feats), BF16),
            pltpu.VMEM((4, rows, feats), BF16),
            pltpu.VMEM((4, rows, block), BF16),
            pltpu.VMEM((4, 2, w_rows, feats), BF16),
            pltpu.VMEM((4, 8, LANES), F32),
            pltpu.VMEM((4, rows, feats), BF16),
            pltpu.VMEM((4, rows, block), F32),
            pltpu.VMEM((4, rows, 1), F32),
            pltpu.VMEM((4, 4, rows, chunk), BF16),
            pltpu.VMEM((4, 4, rows, chunk), F32),
            pltpu.VMEM((4, 4, rows, chunk), F32),
            pltpu.VMEM((4, rows, 1), F32),
            pltpu.VMEM((4, rows, 1), F32),
            pltpu.VMEM((4, rows, block), BF16),
            pltpu.VMEM((4, 8, feats), F32),
            pltpu.VMEM((4, 4, 8, LANES), F32),
            pltpu.VMEM((2, SEQS, block), F32),
            pltpu.VMEM((2, SEQS, lot), F32),
            pltpu.VMEM((SEQS, feats), F32),
            pltpu.VMEM((7, SEQS, lot), F32),
            pltpu.VMEM((4, 3, SEQS, lot), F32),
            pltpu.VMEM((4, 2, 3, SEQS, lot), F32),
            pltpu.VMEM((4, 4, 1, chunk), F32),
            pltpu.VMEM((4, 4, rows, chunk), BF16),
            pltpu.VMEM((4, 4, rows, chunk), BF16),
            pltpu.VMEM((rows, feats), BF16),
            pltpu.VMEM((rows, feats), BF16),
            pltpu.VMEM((8, LANES), F32),
            pltpu.VMEM((8, LANES), F32),
            pltpu.VMEM((4, rows, block), BF16),
            pltpu.VMEM((4, rows * 3 // 8, block), BF16),
            pltpu.SemaphoreType.DMA((COPIES,)),
            pltpu.SemaphoreType.DMA((COPIES,)),
            pltpu.SemaphoreType.DMA((8,)),
        ],
        compiler_params=pltpu.CompilerParams(
            collective_id=0, has_side_effects=True, vmem_limit_bytes=56 * 1024 * 1024
        ),
    )(layer_input[0], out_grad[0], jnp.transpose(modulation[0], (1, 0, 2)), proj_weight[0])
    last = lax.axis_index("section") == sections - 1
    handoff = jnp.where(last, jnp.zeros_like(handoff), handoff)
    return (handoff[None], jnp.transpose(grads, (1, 0, 2))[None])


def solution(mesh):
    in_specs = (
        P("section", "shard", None),
        P("section", "shard", None),
        P("section", None, None, None),
        P("section", "shard", None),
    )
    out_specs = (P("section", "shard", None), P("section", None, None, None))
    return jax.shard_map(
        on_device, mesh=mesh, in_specs=in_specs, out_specs=out_specs, check_vma=False
    )
```

```python
import functools

import jax
import jax.numpy as jnp
from jax import lax
from jax.experimental import pallas as pl
from jax.experimental.pallas import tpu as pltpu
from jax.sharding import PartitionSpec as P

MESH = pl.DeviceIdType.MESH
F32 = jnp.float32
BF16 = jnp.bfloat16

SEQS = 4
OFF = (0, 3, 1, 2)
AWAY = (0, 1, 3, 2)
LANES = 128
COPIES = 96


def stats_to_rows(first, second):
    lane = lax.broadcasted_iota(jnp.int32, (LANES, LANES), 1)
    square = jnp.where(lane == 0, first, jnp.where(lane == 1, second, 0.0))
    return jnp.transpose(square)[:8]


def rows_to_stats(rows):
    square = jnp.concatenate([rows, jnp.zeros((LANES - 8, LANES), F32)], axis=0)
    columns = jnp.transpose(square)
    return columns[:, 0:1], columns[:, 1:2]


def kernel(
    sections, li_ref, og_ref, mod_ref, w_ref, out_ref, mg_ref,
    li_own, og_all, li_all, w_all, st_all, scaled, normed, inv_all, modulated, gm, norm_by, first_sum, second_sum, outgoing,
    gate_acc, sums, part, part_rx, gate_buf, gate_rx, by_z, full, factor, chunk_tx, chunk_rx,
    next_li, next_og, mean_tx, mean_rx, ready, relay, send_sem, recv_sem, local_sem,
):
    rows, feats = og_ref.shape
    block = feats // 4
    chunk = feats // 16
    w_rows = w_ref.shape[0]
    lot = block // 2
    half, w_half = rows // 2, w_rows // 2

    sec = lax.axis_index("section")
    shard = lax.axis_index("shard")
    x = shard // 8
    z = (shard % 8) // 2
    c = shard % 2
    other = 1 - c

    def at_x(k):
        return (sec, lax.rem(x + k, 4) * 8 + z * 2 + c)

    def at_z(dz, dc):
        return (sec, x * 8 + lax.rem(z + dz, 4) * 2 + lax.rem(c + dc, 2))

    def at_plane(k, dc):
        return (sec, lax.rem(x + k, 4) * 8 + z * 2 + lax.rem(c + dc, 2))

    def at_section(step, pos):
        return (sec + step, pos * 8 + z * 2 + c)

    def copy(ident, src, dst, device):
        return pltpu.make_async_remote_copy(
            src_ref=src, dst_ref=dst, send_sem=send_sem.at[ident], recv_sem=recv_sem.at[ident],
            device_id=device, device_id_type=MESH,
        )

    corner = sections // 2
    streams = jnp.logical_and(sec > 0, sec != corner)
    hears = jnp.logical_and(sec < sections - 1, sec != corner - 1)

    ids = iter(range(COPIES))
    slot_x = [lax.rem(x + OFF[n], 4) for n in range(4)]
    plane = [(k, dc) for k in range(4) for dc in range(2) if (k, dc) != (0, 0)]

    def columns(pos):
        return pl.ds(pl.multiple_of(pos * block, LANES), block)

    own_columns = columns(x)

    barrier = pltpu.get_barrier_semaphore()

    def greet(device):
        pl.semaphore_signal(barrier, inc=1, device_id=device, device_id_type=MESH)

    for k, dc in plane:
        greet(at_plane(k, dc))
    for dz in range(1, 4):
        greet(at_z(dz, 0))

    @pl.when(sec > 0)
    def _():
        for pos in range(4):
            greet(at_section(-1, pos))

    @pl.when(sec < sections - 1)
    def _():
        for pos in range(4):
            greet(at_section(1, pos))

    @pl.when(sec == corner)
    def _():
        for pos in range(4):
            greet(at_section(-corner, pos))

    @pl.when(sec == 0)
    def _():
        for pos in range(4):
            greet(at_section(corner, pos))
        greet(at_section(corner - 1, x))

    @pl.when(sec == corner - 1)
    def _():
        greet(at_section(1 - corner, x))

    def one_if(test):
        return jnp.where(test, 1, 0)

    extra = 4 * one_if(sec == corner) + 5 * one_if(sec == 0) + one_if(sec == corner - 1)
    neighbours = (sec + sections - 1) // sections + (2 * sections - 2 - sec) // sections
    pl.semaphore_wait(barrier, 3 + len(plane) + 4 * neighbours + extra)

    low, high = pl.ds(0, half), pl.ds(half, half)
    w_low, w_high = pl.ds(0, w_half), pl.ds(w_half, w_half)
    og_r_low = copy(next(ids), og_ref.at[low], og_all.at[1, low], at_x(1))
    og_r_high = copy(next(ids), og_ref.at[high], og_all.at[1, high], at_x(1))
    og_l_high = copy(next(ids), og_ref.at[high], og_all.at[2, high], at_x(3))
    og_l_low = copy(next(ids), og_ref.at[low], og_all.at[2, low], at_x(3))
    og_fr = copy(next(ids), og_all.at[1, low], og_all.at[3, low], at_x(1))
    og_fl = copy(next(ids), og_all.at[2, high], og_all.at[3, high], at_x(3))
    w_u_low = copy(next(ids), w_ref.at[w_low], w_all.at[1, c, w_low], at_z(1, 0))
    w_u_high = copy(next(ids), w_ref.at[w_high], w_all.at[1, c, w_high], at_z(1, 0))
    w_d_high = copy(next(ids), w_ref.at[w_high], w_all.at[2, c, w_high], at_z(3, 0))
    w_d_low = copy(next(ids), w_ref.at[w_low], w_all.at[2, c, w_low], at_z(3, 0))
    w_fu = copy(next(ids), w_all.at[1, c, w_low], w_all.at[3, c, w_low], at_z(1, 0))
    w_fd = copy(next(ids), w_all.at[2, c, w_high], w_all.at[3, c, w_high], at_z(3, 0))
    li_sends = [
        copy(next(ids), li_ref.at[:, columns(lax.rem(x + AWAY[n], 4))], li_all.at[n], at_x(AWAY[n]))
        for n in (1, 2, 3)
    ]
    st_sends = [copy(next(ids), st_all.at[0], st_all.at[n], at_x(AWAY[n])) for n in (1, 2, 3)]
    own_sib = next(ids)
    w_sib = copy(own_sib, w_ref, w_all.at[0, c], at_z(0, 1))
    w_sib_in = copy(own_sib, w_ref, w_all.at[0, other], at_z(0, 1))

    for step in (og_r_low, og_l_high, w_u_low, w_d_high, og_r_high, og_l_low, w_u_high, w_d_low, w_sib):
        step.start()
    for step in li_sends:
        step.start()
    og_next = copy(next(ids), og_ref, next_og, at_section(-1, x))
    li_next = copy(next(ids), li_ref, next_li, at_section(-1, x))

    @pl.when(streams)
    def _():
        li_next.start()
        og_next.start()

    local = [
        pltpu.make_async_copy(og_ref, og_all.at[0], local_sem.at[0]),
        pltpu.make_async_copy(li_ref, li_own, local_sem.at[1]),
        pltpu.make_async_copy(w_ref, w_all.at[0, c], local_sem.at[2]),
    ]
    for step in local:
        step.start()

    sib_sends, sib_waits = [w_sib], {}

    def to_sibling(slot, part_rows):
        ident = next(ids)
        place = w_all.at[slot, c, part_rows]
        send = copy(ident, place, place, at_z(0, 1))
        send.start()
        sib_sends.append(send)
        sib_waits.setdefault(slot, []).append(copy(ident, place, w_all.at[slot, other, part_rows], at_z(0, 1)))

    for step in local:
        step.wait()
    li_all[0] = li_own[:, own_columns]
    values = li_own[...].astype(F32)
    mean = jnp.sum(values, axis=1, keepdims=True) / feats
    center = values - mean
    variance = jnp.sum(center * center, axis=1, keepdims=True) / feats
    st_all[0] = stats_to_rows(mean, lax.rsqrt(variance + 1e-06))
    for step in st_sends:
        step.start()
    gate_acc[...] = jnp.zeros_like(gate_acc)

    def scale_grad(n):
        gate = mod_ref[2, pl.ds(slot_x[n], 1), :]
        scaled[n] = (gate * og_all[n].astype(F32)).astype(BF16)

    def modulate(n):
        mean_n, inv_n = rows_to_stats(st_all[n])
        inv_all[n] = inv_n
        norm_n = (li_all[n].astype(F32) - mean_n) * inv_n
        normed[n] = norm_n
        scale = mod_ref[1, pl.ds(slot_x[n], 1), own_columns]
        shift = mod_ref[0, pl.ds(slot_x[n], 1), own_columns]
        mod_n = (norm_n * (1.0 + scale) + shift).astype(BF16)
        for j in range(4):
            modulated[j, n] = mod_n[:, j * chunk:(j + 1) * chunk]
            factor[j, n] = 1.0 + scale[:, j * chunk:(j + 1) * chunk]
            norm_by[j, n] = norm_n[:, j * chunk:(j + 1) * chunk]

    scale_grad(0)
    modulate(0)

    og_r_low.wait_recv()
    og_fr.start()
    og_l_high.wait_recv()
    og_fl.start()
    w_u_low.wait_recv()
    w_fu.start()
    to_sibling(1, w_low)
    w_d_high.wait_recv()
    w_fd.start()
    to_sibling(2, w_high)
    og_r_high.wait_recv()
    og_l_low.wait_recv()
    scale_grad(1)
    scale_grad(2)
    for n in (1, 2):
        li_sends[n - 1].wait_recv()
        st_sends[n - 1].wait_recv()
        modulate(n)
    tile = 512

    def chunk_of(slot):
        return lax.rem(z + OFF[slot], 4)

    sum_sends = [copy(next(ids), sums.at[0], sums.at[n], at_x(AWAY[n])) for n in (1, 2, 3)]
    chunk_ids = [[next(ids) for n in range(4)] for slot in range(4)]

    def chunk_copy(slot, n):
        j = chunk_of(slot)
        return copy(chunk_ids[slot][n], chunk_tx.at[n, j], chunk_rx.at[n, j], at_section(-1, slot_x[n]))

    def grad_product(slot, first, count):
        left = scaled[first:first + count].reshape(count * rows, feats)
        right = w_all[slot].reshape(chunk, feats)
        product = lax.dot_general(left, right, (((1,), (1,)), ((), ())), preferred_element_type=F32)
        gm[chunk_of(slot), first:first + count] = product.reshape(count, rows, chunk)
        for n in range(first, first + count):
            grad_norm = gm[chunk_of(slot), n] * factor[chunk_of(slot), n]
            one = jnp.sum(grad_norm, axis=1, keepdims=True)
            two = jnp.sum(grad_norm * norm_by[chunk_of(slot), n], axis=1, keepdims=True)
            if slot == 3:
                sums[0, slot_x[n]] = stats_to_rows(first_sum[n] + one, second_sum[n] + two)
            elif slot == 0:
                first_sum[n] = one
                second_sum[n] = two
            else:
                first_sum[n] += one
                second_sum[n] += two
        if slot == 3:
            for step in sum_sends:
                step.start()

        @pl.when(streams)
        def _():
            for n in range(first, first + count):
                term = inv_all[n] * (gm[chunk_of(slot), n] * factor[chunk_of(slot), n])
                chunk_tx[n, chunk_of(slot)] = term.astype(BF16)
                chunk_copy(slot, n).start()

    def branch_product(slots, first, count):
        def body(step, carry):
            cols = pl.ds(pl.multiple_of(step * tile, tile), tile)
            branch = None
            for slot in slots:
                left = modulated[chunk_of(slot), first:first + count].reshape(count * rows, chunk)
                right = w_all[slot, :, :, cols].reshape(chunk, tile)
                term = jnp.dot(left, right, preferred_element_type=F32)
                branch = term if branch is None else branch + term
            weighed = branch.reshape(count, rows, tile) * og_all[first:first + count, :, cols].astype(F32)
            gate_acc[first:first + count, :, cols] += jnp.sum(
                weighed.reshape(count, rows // 8, 8, tile), axis=1
            )
            return carry

        lax.fori_loop(0, feats // tile, body, 0)

    w_sib_in.wait_recv()
    grad_product(0, 0, 3)
    branch_product((0,), 0, 3)

    w_u_high.wait_recv()
    to_sibling(1, w_high)
    w_d_low.wait_recv()
    to_sibling(2, w_low)
    for slot in (1, 2):
        for step in sib_waits[slot]:
            step.wait_recv()
        grad_product(slot, 0, 3)

    og_fr.wait_recv()
    og_fl.wait_recv()
    scale_grad(3)
    li_sends[2].wait_recv()
    st_sends[2].wait_recv()
    modulate(3)
    for slot in (0, 1, 2):
        grad_product(slot, 3, 1)
    branch_product((1, 2), 0, 3)
    branch_product((0, 1, 2), 3, 1)

    w_fu.wait_recv()
    to_sibling(3, w_low)
    w_fd.wait_recv()
    to_sibling(3, w_high)
    for step in sib_waits[3]:
        step.wait_recv()
    grad_product(3, 0, 4)

    def joined(n):
        return jnp.concatenate([gm[j, n] for j in range(4)], axis=1)

    def place_rows(per_slot):
        row = lax.broadcasted_iota(jnp.int32, (SEQS, per_slot[0].shape[1]), 0)
        total = jnp.zeros(row.shape, F32)
        for n in range(4):
            total = total + jnp.where(row == slot_x[n], per_slot[n], 0.0)
        return total

    branch_product((3,), 0, 4)
    def lot_of(pos, core):
        return pl.ds(pl.multiple_of(pos * block + core * lot, LANES), lot)

    gate_sends = [
        copy(
            next(ids), gate_buf.at[:, lot_of(lax.rem(x + k, 4), lax.rem(c + dc, 2))], gate_rx.at[i],
            at_plane(k, dc),
        )
        for i, (k, dc) in enumerate(plane)
    ]
    def send_gates():
        gate_buf[...] = place_rows([jnp.sum(gate_acc[n], axis=0, keepdims=True) for n in range(4)])
        for step in gate_sends:
            step.start()

    pl.when(sec != corner)(send_gates)

    for step in sum_sends:
        step.wait_recv()
    def row_means(n):
        rows_of = sums[0, slot_x[n]] + sums[1, slot_x[n]] + sums[2, slot_x[n]] + sums[3, slot_x[n]]
        return rows_of

    mean_tx[...] = row_means(0)
    mean_send = copy(next(ids), mean_tx, mean_rx, at_section(-1, x))

    @pl.when(streams)
    def _():
        mean_send.start()

    hand_ids = [next(ids) for n in range(4)]

    def hand(n):
        return copy(hand_ids[n], outgoing.at[n, straight], out_ref.at[straight, own_columns], at_section(-1, slot_x[n]))

    via_ids = [next(ids) for n in range(4)]
    relay_ids = [next(ids) for n in range(4)]
    straight, around = pl.ds(0, rows - relay.shape[1]), pl.ds(rows - relay.shape[1], relay.shape[1])

    def via(n):
        return copy(via_ids[n], outgoing.at[n, around], relay.at[n], at_section(-corner, slot_x[n]))

    def from_columns(n):
        return columns(lax.rem(x + 4 - OFF[n], 4))

    def relayed(n):
        return copy(relay_ids[n], relay.at[n], out_ref.at[around, from_columns(n)], at_section(corner - 1, x))

    def pass_on(*which):
        @pl.when(sec == 0)
        def _():
            for n in which:
                copy(via_ids[n], relay.at[n], relay.at[n], at_section(corner, slot_x[n])).wait_recv()
                relayed(n).start()

    @pl.when(sec == corner)
    def _():
        for n in range(4):
            first, second = rows_to_stats(row_means(n))
            scale = mod_ref[1, pl.ds(slot_x[n], 1), own_columns]
            centered = joined(n) * (1.0 + scale) - first / feats
            grad_in = og_all[n, :, own_columns].astype(F32) + inv_all[n] * (
                centered - normed[n] * (second / feats)
            )
            outgoing[n] = grad_in.astype(BF16)
            via(n).start()
            hand(n).start()

    pl.when(sec == corner)(send_gates)

    zero_copy = pltpu.make_async_copy(scaled.at[0], out_ref, local_sem.at[3])

    @pl.when(sec == sections - 1)
    def _():
        scaled[0] = jnp.zeros_like(scaled[0])
        zero_copy.start()

    shifts, scales = [], []
    for n in range(4):
        grad_mod = joined(n)
        shifts.append(jnp.sum(grad_mod, axis=0, keepdims=True))
        scales.append(jnp.sum(grad_mod * normed[n], axis=0, keepdims=True))
    part[0] = place_rows(shifts)
    part[1] = place_rows(scales)

    part_send = copy(next(ids), part.at[:, :, lot_of(0, other)], part_rx, at_z(0, 1))
    part_send.start()
    for step in gate_sends:
        step.wait_recv()
    gate = gate_buf[:, lot_of(x, c)]
    for i in range(len(plane)):
        gate = gate + gate_rx[i]
    by_z[z, 2] = gate
    part_send.wait_recv()
    by_z[z, 0:2] = part[:, :, lot_of(0, c)] + part_rx[...]
    z_ids = [next(ids) for _ in range(6)]
    edge_plane = lax.rem(sec, corner) == corner - 1

    def round_z(i):
        held = by_z.at[lax.rem(z + 4 - i, 4)]
        return copy(z_ids[i], held, held, at_z(1, 0))

    def across_z(i):
        return copy(z_ids[3 + i], by_z.at[z], by_z.at[z], at_z(i + 1, 0))

    @pl.when(edge_plane)
    def _():
        for i in range(3):
            round_z(i).start()
            landed = by_z.at[lax.rem(z + 3 - i, 4)]
            copy(z_ids[i], landed, landed, at_z(1, 0)).wait_recv()

    @pl.when(jnp.logical_not(edge_plane))
    def _():
        for i in range(3):
            across_z(i).start()
        pass_on(0)
        for i in range(3):
            landed = by_z.at[lax.rem(z + 3 - i, 4)]
            copy(z_ids[3 + i], landed, landed, at_z(i + 1, 0)).wait_recv()

    full[x, c] = by_z[0] + by_z[1] + by_z[2] + by_z[3]
    full_ids = [next(ids) for _ in plane]
    full_sends = [
        copy(full_ids[i], full.at[x, c], full.at[x, c], at_plane(k, dc)) for i, (k, dc) in enumerate(plane)
    ]
    for step in full_sends:
        step.start()
    pass_on(1, 2)

    def finished(n):
        return pltpu.make_async_copy(ready.at[n], out_ref.at[:, from_columns(n)], local_sem.at[4 + n])

    @pl.when(hears)
    def _():
        li_next.wait_recv()
        later = next_li[...].astype(F32)
        later_mean = jnp.sum(later, axis=1, keepdims=True) / feats
        later_center = later - later_mean
        later_inv = lax.rsqrt(jnp.sum(later_center * later_center, axis=1, keepdims=True) / feats + 1e-06)
        og_next.wait_recv()
        mean_send.wait_recv()
        first, second = rows_to_stats(mean_rx[...])
        for n in range(4):
            for slot in range(4):
                chunk_copy(slot, n).wait_recv()
            cols = from_columns(n)
            term = jnp.concatenate([chunk_rx[n, j].astype(F32) for j in range(4)], axis=1)
            norm_n = (next_li[:, cols].astype(F32) - later_mean) * later_inv
            taken = later_inv * (first / feats + norm_n * (second / feats))
            ready[n] = (next_og[:, cols].astype(F32) + (term - taken)).astype(BF16)
            finished(n).start()

    pass_on(3)
    for i, (k, dc) in enumerate(plane):
        landed = full.at[lax.rem(x + 4 - k, 4), lax.rem(c + dc, 2)]
        copy(full_ids[i], landed, landed, at_plane(k, dc)).wait_recv()
    for pos in range(4):
        for core in range(2):
            start = pos * block + core * lot
            mg_ref[:, :, start:start + lot] = full[pos, core]

    for step in (
        og_r_low, og_r_high, og_l_high, og_l_low, og_fr, og_fl, w_u_low, w_u_high, w_d_high, w_d_low,
        w_fu, w_fd, *li_sends, *st_sends, *sib_sends, *sum_sends, *gate_sends, part_send, *full_sends,
    ):
        step.wait_send()
    @pl.when(edge_plane)
    def _():
        for i in range(3):
            round_z(i).wait_send()

    @pl.when(jnp.logical_not(edge_plane))
    def _():
        for i in range(3):
            across_z(i).wait_send()

    @pl.when(streams)
    def _():
        og_next.wait_send()
        li_next.wait_send()
        mean_send.wait_send()
        for slot in range(4):
            for n in range(4):
                chunk_copy(slot, n).wait_send()

    @pl.when(hears)
    def _():
        for n in range(4):
            finished(n).wait()

    @pl.when(sec == corner)
    def _():
        for n in range(4):
            hand(n).wait_send()
            via(n).wait_send()

    @pl.when(sec == 0)
    def _():
        for n in range(4):
            relayed(n).wait_send()

    @pl.when(sec == corner - 1)
    def _():
        for n in range(4):
            landed = out_ref.at[straight, from_columns(n)]
            copy(hand_ids[n], outgoing.at[n, straight], landed, at_section(1, slot_x[n])).wait_recv()
            landed = out_ref.at[around, from_columns(n)]
            copy(relay_ids[n], relay.at[n], landed, at_section(1 - corner, x)).wait_recv()

    @pl.when(sec == sections - 1)
    def _():
        zero_copy.wait()


def on_device(layer_input, out_grad, modulation, proj_weight):
    sections = lax.axis_size("section")
    rows, feats = layer_input.shape[1:]
    w_rows = proj_weight.shape[1]
    block, chunk = feats // 4, feats // 16
    lot = block // 2
    vmem = pl.BlockSpec(memory_space=pltpu.VMEM)
    anywhere = pl.BlockSpec(memory_space=pl.ANY)
    handoff, grads = pl.pallas_call(
        functools.partial(kernel, sections),
        out_shape=(
            jax.ShapeDtypeStruct((rows, feats), BF16),
            jax.ShapeDtypeStruct((3, SEQS, feats), F32),
        ),
        in_specs=[anywhere, anywhere, vmem, anywhere],
        out_specs=(anywhere, vmem),
        scratch_shapes=[
            pltpu.VMEM((rows, feats), BF16),
            pltpu.VMEM((4, rows, feats), BF16),
            pltpu.VMEM((4, rows, block), BF16),
            pltpu.VMEM((4, 2, w_rows, feats), BF16),
            pltpu.VMEM((4, 8, LANES), F32),
            pltpu.VMEM((4, rows, feats), BF16),
            pltpu.VMEM((4, rows, block), F32),
            pltpu.VMEM((4, rows, 1), F32),
            pltpu.VMEM((4, 4, rows, chunk), BF16),
            pltpu.VMEM((4, 4, rows, chunk), F32),
            pltpu.VMEM((4, 4, rows, chunk), F32),
            pltpu.VMEM((4, rows, 1), F32),
            pltpu.VMEM((4, rows, 1), F32),
            pltpu.VMEM((4, rows, block), BF16),
            pltpu.VMEM((4, 8, feats), F32),
            pltpu.VMEM((4, 4, 8, LANES), F32),
            pltpu.VMEM((2, SEQS, block), F32),
            pltpu.VMEM((2, SEQS, lot), F32),
            pltpu.VMEM((SEQS, feats), F32),
            pltpu.VMEM((7, SEQS, lot), F32),
            pltpu.VMEM((4, 3, SEQS, lot), F32),
            pltpu.VMEM((4, 2, 3, SEQS, lot), F32),
            pltpu.VMEM((4, 4, 1, chunk), F32),
            pltpu.VMEM((4, 4, rows, chunk), BF16),
            pltpu.VMEM((4, 4, rows, chunk), BF16),
            pltpu.VMEM((rows, feats), BF16),
            pltpu.VMEM((rows, feats), BF16),
            pltpu.VMEM((8, LANES), F32),
            pltpu.VMEM((8, LANES), F32),
            pltpu.VMEM((4, rows, block), BF16),
            pltpu.VMEM((4, rows * 3 // 8, block), BF16),
            pltpu.SemaphoreType.DMA((COPIES,)),
            pltpu.SemaphoreType.DMA((COPIES,)),
            pltpu.SemaphoreType.DMA((8,)),
        ],
        compiler_params=pltpu.CompilerParams(
            collective_id=0, has_side_effects=True, vmem_limit_bytes=52 * 1024 * 1024
        ),
    )(layer_input[0], out_grad[0], jnp.transpose(modulation[0], (1, 0, 2)), proj_weight[0])
    last = lax.axis_index("section") == sections - 1
    handoff = jnp.where(last, jnp.zeros_like(handoff), handoff)
    return (handoff[None], jnp.transpose(grads, (1, 0, 2))[None])


def solution(mesh):
    in_specs = (
        P("section", "shard", None),
        P("section", "shard", None),
        P("section", None, None, None),
        P("section", "shard", None),
    )
    out_specs = (P("section", "shard", None), P("section", None, None, None))
    return jax.shard_map(
        on_device, mesh=mesh, in_specs=in_specs, out_specs=out_specs, check_vma=False
    )
```
